32 devices in a mesh: dp: 16 (over z, y, core), tensor: 2 (over x).
Axes of the slice: x: 2, y: 2, z: 4, core: 2. Of those that a mesh axis runs over, the one named last changes fastest.
Arguments:
- latents_in: bfloat16 [16, 1024, 1152], P('dp', 'tensor'), may hold values from -6 to 6
- steps: int32 [16], P('dp'), may hold values from 0 to 999
- labels: int32 [16], P('dp'), may hold values from 0 to 999
- class_table: bfloat16 [1000, 1152], P(None, 'tensor'), may hold values from -6 to 6
- w_ada: bfloat16 [1152, 6912], P('tensor', 'dp'), may hold values from -0.1875 to 0.1875
- w_qkv: bfloat16 [3, 1152, 1152], P(None, 'dp', 'tensor'), may hold values from -0.1875 to 0.1875
- w_proj: bfloat16 [1152, 1152], P('tensor', 'dp'), may hold values from -3 to 3
- w_fc1: bfloat16 [1152, 4608], P('dp', 'tensor'), may hold values from -0.1875 to 0.1875
- w_fc2: bfloat16 [4608, 1152], P('tensor', 'dp'), may hold values from -0.09375 to 0.09375
- cotangent: bfloat16 [16, 1024, 1152], P('dp', 'tensor'), may hold values from -6 to 6
Outputs:
- block_out: bfloat16 [16, 1024, 1152], P('dp', 'tensor')
- grad_latents: float32 [16, 1024, 1152], P('dp', 'tensor')
- grad_class_table: float32 [1000, 1152], P(None, 'tensor')
- grad_w_ada: float32 [1152, 6912], P('tensor', 'dp')
- grad_w_qkv: float32 [3, 1152, 1152], P(None, 'dp', 'tensor')
- grad_w_proj: float32 [1152, 1152], P('tensor', 'dp')
- grad_w_fc1: float32 [1152, 4608], P('dp', 'tensor')
- grad_w_fc2: float32 [4608, 1152], P('tensor', 'dp')
The draws below stay inside these ranges and needn't reach their ends.
All inputs are finite; a program needn't handle non-finite values.
Results may differ from the reference program's by a relative error of at most 0.02.
Values may be sent and summed in bfloat16 or wider, within the bound.
A program may use at most 192 MiB of HBM per device.

```python
import math
import jax
import jax.numpy as jnp
from jax import lax

D = 1152
H = 16
FF = 4608
NCLS = 1000
TOK = 1024
LATENTS = 16


def draw_latents_in(key, part):
    base = jnp.clip(jax.random.normal(key, (LATENTS, TOK, D), jnp.float32), -6.0, 6.0)
    return base.astype(jnp.bfloat16)


def touch_ends(drawn, stream_key, least, high):
    longest = drawn.shape.index(max(drawn.shape))
    spots = []
    for shift in (0, 1):
        where = [jax.random.randint(jax.random.fold_in(stream_key, axis), (), 0, length) for axis, length in enumerate(drawn.shape)]
        where[longest] = (where[longest] + shift) % drawn.shape[longest]
        spots.append(tuple(where))
    return drawn.at[spots[0]].set(least).at[spots[1]].set(high)


def spiked(entries, stream_key, source, target, shards_of, factor):
    def block_of(position):
        return (jnp.arange(entries.shape[position]) // (entries.shape[position] // shards_of)).reshape((-1,) + (1,) * (entries.ndim - 1 - position))

    near = jax.random.permutation(stream_key, shards_of)[block_of(target)]
    far = (block_of(target) + shards_of // 2) % shards_of
    return jnp.where((block_of(source) == near) | (block_of(source) == far), factor * entries, entries)


def steps_of(rng, extent, split, low, high):
    loudness, own = 1.0, jax.random.fold_in(rng, 6)
    for axis_at, parts in split:
        steps = jnp.exp(jax.random.uniform(jax.random.fold_in(own, axis_at), (parts,), jnp.float32, low / len(split), high / len(split)))
        loudness = loudness * jnp.repeat(steps, extent[axis_at] // parts).reshape([-1 if axis == axis_at else 1 for axis in range(len(extent))])
    return loudness


def normal_values(rng, extent, scale, reach, cuts=(), kind=jnp.bfloat16):
    loudness = steps_of(rng, extent, cuts, -0.22, 0.18) if cuts else 1.0
    entries = jax.random.normal(rng, extent, jnp.float32) * scale * loudness
    return jnp.minimum(jnp.maximum(entries, -reach), reach).astype(kind)


def heavy_noise(rng, dims, scale, bound, cuts, heavy, held_as=jnp.bfloat16):
    array = scale * jax.random.normal(rng, dims, jnp.float32)
    if cuts:
        array = array * steps_of(rng, dims, cuts, -0.22, 0.18)
    return jnp.clip(spiked(array, jax.random.fold_in(rng, 3), *heavy), -bound, bound).astype(held_as)


def setup_inputs(seed: int = 0) -> dict:
    key_of = jax.random.split(jax.random.key(seed), 11)
    latents_in = draw_latents_in(jax.random.fold_in(key_of[10], 71), 0)
    steps = touch_ends(jax.random.randint(key_of[1], (LATENTS,), 0, 1000), jax.random.fold_in(key_of[1], 1), 0, 999).astype(jnp.int32)
    labels = touch_ends(jax.random.randint(key_of[2], (LATENTS,), 0, NCLS), jax.random.fold_in(key_of[2], 1), 0, NCLS - 1).astype(jnp.int32)
    class_table = normal_values(key_of[3], (NCLS, D), 1.0, 6.0, ((1, 2),))
    w_ada = normal_values(key_of[4], (D, 6 * D), D ** -0.5, 0.1875, ((0, 2), (1, 16)))
    w_qkv = normal_values(key_of[5], (3, D, D), D ** -0.5, 0.1875, ((1, 16), (2, 2)))
    w_proj = normal_values(key_of[6], (D, D), (max(1, D // 256)) ** -0.5, 3.0, ((0, 2), (1, 16)))
    w_fc1 = normal_values(key_of[7], (D, FF), D ** -0.5, 0.1875, ((0, 16), (1, 2)))
    w_fc2 = normal_values(key_of[8], (FF, D), FF ** -0.5, 0.09375, ((0, 2), (1, 16)))
    cotangent = heavy_noise(key_of[9], (LATENTS, TOK, D), 1.0, 6.0, ((0, 16), (1, 2)), (0, 2, 16, 2.0))
    return {"latents_in": latents_in, "steps": steps, "labels": labels, "class_table": class_table, "w_ada": w_ada, "w_qkv": w_qkv, "w_proj": w_proj, "w_fc1": w_fc1, "w_fc2": w_fc2, "cotangent": cotangent}


norm_epsilon = 1e-06
gelu_factor = 0.7978845608028654
gelu_cubic = 0.044715

def norm_rows(rows):
    average = lax.optimization_barrier(jnp.mean(rows, axis=-1, keepdims=True))
    centred = rows - average
    variance = lax.optimization_barrier(jnp.mean(centred * centred, axis=-1, keepdims=True))
    inv_std = lax.rsqrt(variance + norm_epsilon)
    return (centred * inv_std, inv_std)

def norm_back(grad_normed, normed, inv_std):
    first = lax.optimization_barrier(jnp.mean(grad_normed, axis=-1, keepdims=True))
    second = lax.optimization_barrier(jnp.mean(grad_normed * normed, axis=-1, keepdims=True))
    return inv_std * (grad_normed - first - normed * second)

def gelu_value(pre):
    inner = gelu_factor * (pre + gelu_cubic * pre * pre * pre)
    return 0.5 * pre * (1.0 + jnp.tanh(inner))

def gelu_slope(pre):
    tangent = jnp.tanh(gelu_factor * (pre + gelu_cubic * pre * pre * pre))
    return 0.5 * (1.0 + tangent) + 0.5 * pre * (1.0 - tangent * tangent) * gelu_factor * (1.0 + 3.0 * gelu_cubic * pre * pre)

def silu_value(value):
    return value * jax.nn.sigmoid(value)

def silu_slope(value):
    sigma = jax.nn.sigmoid(value)
    return sigma * (1.0 + value * (1.0 - sigma))

def time_columns(steps_float, columns, width):
    half = width // 2
    index = jnp.where(columns < half, columns, columns - half).astype(jnp.float32)
    freqs = jnp.exp(-math.log(10000.0) * index / half)
    angles = steps_float[:, None] * freqs[None, :]
    return jnp.where(columns[None, :] < half, jnp.cos(angles), jnp.sin(angles))

def widen(value):
    return lax.optimization_barrier(value).astype(jnp.float32)

def reference(latents_in, steps, labels, class_table, w_ada, w_qkv, w_proj, w_fc1, w_fc2, cotangent):
    head_size = D // H
    score_scale = head_size ** (-0.5)
    columns = jnp.arange(D, dtype=jnp.int32)
    highest = lax.Precision.HIGHEST

    def latent(carry, items):
        acc_table, acc_ada, acc_qkv, acc_proj, acc_fc1, acc_fc2 = carry
        rows_half, step_one, label_one, cot_half = items
        rows_in = rows_half.astype(jnp.float32)
        cond = time_columns(step_one.astype(jnp.float32).reshape(1), columns, D) + class_table[label_one].astype(jnp.float32)[None, :]
        cond_half = silu_value(cond).astype(jnp.bfloat16)
        modulation = jnp.dot(cond_half, w_ada, preferred_element_type=jnp.float32).reshape(6, D)
        shift_a, scale_a, gate_a = (modulation[0], modulation[1], modulation[2])
        shift_m, scale_m, gate_m = (modulation[3], modulation[4], modulation[5])
        normed_a, inv_a = norm_rows(rows_in)
        mod_a = (normed_a * (1.0 + scale_a) + shift_a).astype(jnp.bfloat16)
        queries = jnp.dot(mod_a, w_qkv[0], preferred_element_type=jnp.float32).astype(jnp.bfloat16)
        keys = jnp.dot(mod_a, w_qkv[1], preferred_element_type=jnp.float32).astype(jnp.bfloat16)
        values = jnp.dot(mod_a, w_qkv[2], preferred_element_type=jnp.float32).astype(jnp.bfloat16)
        query_wide = widen(queries).reshape(TOK, H, head_size)
        key_wide = widen(keys).reshape(TOK, H, head_size)
        value_wide = widen(values).reshape(TOK, H, head_size)
        scores = jnp.einsum('qhd,khd->hqk', query_wide, key_wide) * score_scale
        largest = lax.optimization_barrier(jnp.max(scores, axis=-1, keepdims=True))
        log_total = largest + jnp.log(lax.optimization_barrier(jnp.sum(jnp.exp(scores - largest), axis=-1, keepdims=True)))
        probs = jnp.exp(scores - log_total).astype(jnp.bfloat16)
        probs_wide = widen(probs)
        mixed = jnp.einsum('hqk,khd->qhd', probs_wide, value_wide).astype(jnp.bfloat16).reshape(TOK, D)
        attn_out = jnp.dot(mixed, w_proj, preferred_element_type=jnp.float32)
        hidden = rows_in + gate_a * attn_out
        normed_m, inv_m = norm_rows(hidden)
        mod_m = (normed_m * (1.0 + scale_m) + shift_m).astype(jnp.bfloat16)
        pre_act = jnp.dot(mod_m, w_fc1, preferred_element_type=jnp.float32)
        acts = gelu_value(pre_act).astype(jnp.bfloat16)
        mlp_out = jnp.dot(acts, w_fc2, preferred_element_type=jnp.float32)
        block_out = (hidden + gate_m * mlp_out).astype(jnp.bfloat16)
        grad_out = cot_half.astype(jnp.float32)
        grad_gate_m = lax.optimization_barrier(jnp.sum(grad_out * mlp_out, axis=0))
        grad_mlp = (grad_out * gate_m).astype(jnp.bfloat16)
        acc_fc2 = acc_fc2 + jnp.dot(acts.T, grad_mlp, preferred_element_type=jnp.float32)
        grad_pre = (jnp.dot(grad_mlp, w_fc2.T, preferred_element_type=jnp.float32) * gelu_slope(pre_act)).astype(jnp.bfloat16)
        acc_fc1 = acc_fc1 + jnp.dot(mod_m.T, grad_pre, preferred_element_type=jnp.float32)
        grad_mod_m = jnp.dot(grad_pre, w_fc1.T, preferred_element_type=jnp.float32)
        grad_shift_m = lax.optimization_barrier(jnp.sum(grad_mod_m, axis=0))
        grad_scale_m = lax.optimization_barrier(jnp.sum(grad_mod_m * normed_m, axis=0))
        grad_hidden = grad_out + norm_back(grad_mod_m * (1.0 + scale_m), normed_m, inv_m)
        grad_gate_a = lax.optimization_barrier(jnp.sum(grad_hidden * attn_out, axis=0))
        grad_attn = (grad_hidden * gate_a).astype(jnp.bfloat16)
        acc_proj = acc_proj + jnp.dot(mixed.T, grad_attn, preferred_element_type=jnp.float32)
        grad_mixed = jnp.dot(grad_attn, w_proj.T, preferred_element_type=jnp.float32).astype(jnp.bfloat16)
        grad_mixed_wide = widen(grad_mixed).reshape(TOK, H, head_size)
        mixed_wide = widen(mixed).reshape(TOK, H, head_size)
        probs_again = jnp.exp(scores - log_total)
        grad_probs = jnp.einsum('qhd,khd->hqk', grad_mixed_wide, value_wide)
        delta = lax.optimization_barrier(jnp.sum(grad_mixed_wide * mixed_wide, axis=-1))
        grad_scores = (probs_again * (grad_probs - jnp.swapaxes(delta, 0, 1)[:, :, None]) * score_scale).astype(jnp.bfloat16)
        grad_scores_wide = widen(grad_scores)
        grad_queries = jnp.einsum('hqk,khd->qhd', grad_scores_wide, key_wide).astype(jnp.bfloat16)
        grad_keys = jnp.einsum('hqk,qhd->khd', grad_scores_wide, query_wide).astype(jnp.bfloat16)
        grad_values = jnp.einsum('hqk,qhd->khd', probs_wide, grad_mixed_wide).astype(jnp.bfloat16)
        grad_qkv = jnp.stack([grad_queries, grad_keys, grad_values]).reshape(3, TOK, D)
        acc_qkv = acc_qkv + jnp.einsum('td,jtc->jdc', widen(mod_a), widen(grad_qkv))
        grad_mod_a = jnp.einsum('jtc,jdc->td', widen(grad_qkv), w_qkv.astype(jnp.float32))
        grad_shift_a = lax.optimization_barrier(jnp.sum(grad_mod_a, axis=0))
        grad_scale_a = lax.optimization_barrier(jnp.sum(grad_mod_a * normed_a, axis=0))
        grad_input = grad_hidden + norm_back(grad_mod_a * (1.0 + scale_a), normed_a, inv_a)
        grad_modulation = jnp.stack([grad_shift_a, grad_scale_a, grad_gate_a, grad_shift_m, grad_scale_m, grad_gate_m]).reshape(1, 6 * D)
        acc_ada = acc_ada + jnp.dot(widen(cond_half).T, grad_modulation, precision=highest)
        grad_cond = jnp.dot(grad_modulation, w_ada.astype(jnp.float32).T, precision=highest) * silu_slope(cond)
        acc_table = acc_table.at[label_one].add(grad_cond[0])
        return ((acc_table, acc_ada, acc_qkv, acc_proj, acc_fc1, acc_fc2), (block_out, grad_input))
    start = (jnp.zeros((NCLS, D), jnp.float32), jnp.zeros((D, 6 * D), jnp.float32), jnp.zeros((3, D, D), jnp.float32), jnp.zeros((D, D), jnp.float32), jnp.zeros((D, FF), jnp.float32), jnp.zeros((FF, D), jnp.float32))
    finals, outputs = lax.scan(latent, start, (latents_in, steps, labels, cotangent))
    acc_table, acc_ada, acc_qkv, acc_proj, acc_fc1, acc_fc2 = finals
    block_out, grad_latents = outputs
    return (block_out, grad_latents, acc_table, acc_ada, acc_qkv, acc_proj, acc_fc1, acc_fc2)
```

```python
import functools
import math

import jax
import jax.numpy as jnp
from jax import lax
from jax.sharding import PartitionSpec as P

D = 1152
H = 16


norm_epsilon = 1e-06
gelu_factor = 0.7978845608028654
gelu_cubic = 0.044715


def norm_rows(rows):
    average = jnp.mean(rows, axis=-1, keepdims=True)
    centred = rows - average
    variance = jnp.mean(centred * centred, axis=-1, keepdims=True)
    inv_std = lax.rsqrt(variance + norm_epsilon)
    return (centred * inv_std, inv_std)


def norm_back(grad_normed, normed, inv_std):
    first = jnp.mean(grad_normed, axis=-1, keepdims=True)
    second = jnp.mean(grad_normed * normed, axis=-1, keepdims=True)
    return inv_std * (grad_normed - first - normed * second)


def gelu_value(pre):
    inner = gelu_factor * (pre + gelu_cubic * pre * pre * pre)
    return 0.5 * pre * (1.0 + jnp.tanh(inner))


def gelu_slope(pre):
    tangent = jnp.tanh(gelu_factor * (pre + gelu_cubic * pre * pre * pre))
    return 0.5 * (1.0 + tangent) + 0.5 * pre * (1.0 - tangent * tangent) * gelu_factor * (
        1.0 + 3.0 * gelu_cubic * pre * pre
    )


def silu_value(value):
    return value * jax.nn.sigmoid(value)


def silu_slope(value):
    sigma = jax.nn.sigmoid(value)
    return sigma * (1.0 + value * (1.0 - sigma))


def time_columns(steps_float, columns, width):
    half = width // 2
    index = jnp.where(columns < half, columns, columns - half).astype(jnp.float32)
    freqs = jnp.exp(-math.log(10000.0) * index / half)
    angles = steps_float[:, None] * freqs[None, :]
    return jnp.where(columns[None, :] < half, jnp.cos(angles), jnp.sin(angles))


def attend(queries, keys, values, score_scale):
    scores = (
        jnp.einsum("qhd,khd->hqk", queries, keys, preferred_element_type=jnp.float32) * score_scale
    )
    largest = jnp.max(scores, axis=-1, keepdims=True)
    log_total = largest + jnp.log(jnp.sum(jnp.exp(scores - largest), axis=-1, keepdims=True))
    probs = jnp.exp(scores - log_total).astype(jnp.bfloat16)
    mixed = jnp.einsum("hqk,khd->qhd", probs, values, preferred_element_type=jnp.float32)
    return (mixed.astype(jnp.bfloat16), log_total[:, :, 0])


def attend_back(queries, keys, values, mixed, grad_mixed, log_totals, score_scale):
    scores = (
        jnp.einsum("qhd,khd->hqk", queries, keys, preferred_element_type=jnp.float32) * score_scale
    )
    probs = jnp.exp(scores - log_totals[:, :, None])
    grad_values = jnp.einsum(
        "hqk,qhd->khd", probs.astype(jnp.bfloat16), grad_mixed, preferred_element_type=jnp.float32
    )
    grad_probs = jnp.einsum("qhd,khd->hqk", grad_mixed, values, preferred_element_type=jnp.float32)
    delta = jnp.sum(grad_mixed.astype(jnp.float32) * mixed.astype(jnp.float32), axis=-1)
    grad_scores = (
        probs * (grad_probs - jnp.swapaxes(delta, 0, 1)[:, :, None]) * score_scale
    ).astype(jnp.bfloat16)
    grad_queries = jnp.einsum("hqk,khd->qhd", grad_scores, keys, preferred_element_type=jnp.float32)
    grad_keys = jnp.einsum("hqk,qhd->khd", grad_scores, queries, preferred_element_type=jnp.float32)
    return (grad_queries, grad_keys, grad_values)


def from_rank(value, ranks, step):
    return lax.ppermute(value, "tensor", [(i, (i - step) % ranks) for i in range(ranks)])


def fetch_rest(rows, ranks):
    got = [from_rank(rows, ranks, step) for step in range(1, ranks)]
    return got[0] if ranks == 2 else jnp.concatenate(got, axis=0)


def return_rest(partial, ranks):
    size = partial.shape[0] // (ranks - 1)
    total = None
    for step in range(1, ranks):
        part = partial[(step - 1) * size : step * size].astype(jnp.bfloat16)
        part = from_rank(part, ranks, ranks - step).astype(jnp.float32)
        total = part if total is None else total + part
    return total


def sum_ranks(value, ranks):
    total = value
    for step in range(1, ranks):
        total = total + from_rank(value, ranks, step)
    return total


def dot(spec, left, right):
    return jnp.einsum(spec, left, right, preferred_element_type=jnp.float32)


def join(own, rest):
    return jnp.concatenate([own, rest], axis=0)


def shards(
    ranks, latents_in, steps, labels, class_table, w_ada, w_qkv, w_proj, w_fc1, w_fc2, cotangent
):
    half = jnp.bfloat16
    rank = lax.axis_index("tensor")
    width = latents_in.shape[2]
    mine = latents_in.shape[1]
    owned = class_table.shape[1]
    head_size = D // H
    heads_here = owned // head_size
    score_scale = head_size ** (-0.5)
    highest = lax.Precision.HIGHEST
    marks = lax.all_gather(jnp.stack([steps, labels], axis=1), "dp", axis=0, tiled=True)
    all_steps, all_labels = marks[:, 0], marks[:, 1]
    attn_w = lax.all_gather(
        jnp.concatenate([w_qkv[0], w_qkv[1], w_qkv[2], w_proj.T], axis=1),
        "dp",
        axis=0,
        tiled=True,
    )
    mlp_w = lax.all_gather(jnp.concatenate([w_fc1, w_fc2.T], axis=1), "dp", axis=0, tiled=True)
    qkv_full, proj_t = attn_w[:, : 3 * owned], attn_w[:, 3 * owned :]
    fc1_full, fc2_t = mlp_w[:, : w_fc1.shape[1]], mlp_w[:, w_fc1.shape[1] :]
    columns = rank * owned + jnp.arange(owned, dtype=jnp.int32)
    classes = jnp.arange(class_table.shape[0], dtype=jnp.int32)
    one_hot = (all_labels[:, None] == classes[None, :]).astype(half)
    cond = time_columns(all_steps.astype(jnp.float32), columns, D) + jnp.dot(
        one_hot, class_table, preferred_element_type=jnp.float32
    )
    cond_half = silu_value(cond).astype(half)
    mod_part = jnp.dot(cond_half, w_ada, preferred_element_type=jnp.float32)
    modulation = lax.all_to_all(sum_ranks(mod_part, ranks), "dp", 0, 0, tiled=True)
    modulation = modulation.reshape(6, width)
    shift_a, scale_a, gate_a = (modulation[0], modulation[1], modulation[2])
    shift_m, scale_m, gate_m = (modulation[3], modulation[4], modulation[5])
    rows_in = latents_in[0].astype(jnp.float32)
    normed_a, inv_a = norm_rows(rows_in)
    mod_a = (normed_a * (1.0 + scale_a) + shift_a).astype(half)
    rest_a = fetch_rest(mod_a, ranks)
    grad_out = cotangent[0].astype(jnp.float32)
    grad_mlp = (grad_out * gate_m).astype(half)
    rest_grad_m = fetch_rest(grad_mlp, ranks)
    qkv_own = dot("td,dc->tc", mod_a, qkv_full).astype(half)
    qkv_rest = dot("td,dc->tc", rest_a, qkv_full).astype(half)
    projected = join(qkv_own, qkv_rest)
    tokens = projected.shape[0]
    queries = projected[:, :owned].reshape(tokens, heads_here, head_size)
    keys = projected[:, owned : 2 * owned].reshape(tokens, heads_here, head_size)
    values = projected[:, 2 * owned :].reshape(tokens, heads_here, head_size)
    mixed_rest, log_rest = attend(queries[mine:], keys, values, score_scale)
    mixed_rest_flat = mixed_rest.reshape(tokens - mine, owned)
    attn_away = return_rest(dot("tc,dc->td", mixed_rest_flat, proj_t), ranks)
    mixed_own, log_own = attend(queries[:mine], keys, values, score_scale)
    mixed_own_flat = mixed_own.reshape(mine, owned)
    attn_out = dot("tc,dc->td", mixed_own_flat, proj_t) + attn_away
    hidden = rows_in + gate_a * attn_out
    normed_m, inv_m = norm_rows(hidden)
    mod_m = (normed_m * (1.0 + scale_m) + shift_m).astype(half)
    rest_m = fetch_rest(mod_m, ranks)
    pre_own = dot("td,df->tf", mod_m, fc1_full)
    acts_own = gelu_value(pre_own).astype(half)
    pre_rest = dot("td,df->tf", rest_m, fc1_full)
    acts_rest = gelu_value(pre_rest).astype(half)
    mlp_away = return_rest(dot("tf,df->td", acts_rest, fc2_t), ranks)
    grad_pre_rest = (dot("td,df->tf", rest_grad_m, fc2_t) * gelu_slope(pre_rest)).astype(half)
    grad_mod_away = return_rest(dot("tf,df->td", grad_pre_rest, fc1_full), ranks)
    mlp_out = dot("tf,df->td", acts_own, fc2_t) + mlp_away
    block_out = (hidden + gate_m * mlp_out).astype(half)
    grad_gate_m = jnp.sum(grad_out * mlp_out, axis=0)
    grad_pre_own = (dot("td,df->tf", grad_mlp, fc2_t) * gelu_slope(pre_own)).astype(half)
    grad_mod_m = dot("tf,df->td", grad_pre_own, fc1_full) + grad_mod_away
    grad_fc2_t = dot("td,tf->df", join(grad_mlp, rest_grad_m), join(acts_own, acts_rest))
    grad_fc1 = dot("td,tf->df", join(mod_m, rest_m), join(grad_pre_own, grad_pre_rest))
    mlp_w_part = jnp.concatenate([grad_fc1.astype(half), grad_fc2_t.astype(half)], axis=1)
    mlp_w_part, grad_mod_m = lax.optimization_barrier((mlp_w_part, grad_mod_m))
    grad_mlp_w = lax.psum_scatter(
        mlp_w_part,
        "dp",
        scatter_dimension=0,
        tiled=True,
    ).astype(jnp.float32)
    grad_shift_m = jnp.sum(grad_mod_m, axis=0)
    grad_scale_m = jnp.sum(grad_mod_m * normed_m, axis=0)
    grad_hidden = grad_out + norm_back(grad_mod_m * (1.0 + scale_m), normed_m, inv_m)
    grad_gate_a = jnp.sum(grad_hidden * attn_out, axis=0)
    grad_attn = (grad_hidden * gate_a).astype(half)
    rest_grad_a = fetch_rest(grad_attn, ranks)
    grad_mixed_own = dot("td,dc->tc", grad_attn, proj_t).astype(half)
    grad_mixed_rest = dot("td,dc->tc", rest_grad_a, proj_t).astype(half)
    mixed_flat = join(mixed_own_flat, mixed_rest_flat)
    grad_proj_t = dot("td,tc->dc", join(grad_attn, rest_grad_a), mixed_flat)
    grad_mixed = join(grad_mixed_own, grad_mixed_rest)
    grads = attend_back(
        queries,
        keys,
        values,
        mixed_flat.reshape(tokens, heads_here, head_size),
        grad_mixed.reshape(tokens, heads_here, head_size),
        jnp.concatenate([log_own, log_rest], axis=1),
        score_scale,
    )
    grad_qkv = jnp.concatenate([g.astype(half).reshape(tokens, owned) for g in grads], axis=1)
    grad_a_away = return_rest(dot("tc,dc->td", grad_qkv[mine:], qkv_full), ranks)
    grad_w_qkv = dot("td,tc->dc", join(mod_a, rest_a), grad_qkv)
    attn_w_part = jnp.concatenate([grad_w_qkv.astype(half), grad_proj_t.astype(half)], axis=1)
    attn_w_part, grad_mlp_w = lax.optimization_barrier((attn_w_part, grad_mlp_w))
    grad_attn_w = lax.psum_scatter(
        attn_w_part,
        "dp",
        scatter_dimension=0,
        tiled=True,
    ).astype(jnp.float32)
    grad_mod_a = dot("tc,dc->td", grad_qkv[:mine], qkv_full) + grad_a_away
    grad_shift_a = jnp.sum(grad_mod_a, axis=0)
    grad_scale_a = jnp.sum(grad_mod_a * normed_a, axis=0)
    grad_input = grad_hidden + norm_back(grad_mod_a * (1.0 + scale_a), normed_a, inv_a)
    grad_mod_part = jnp.stack(
        [grad_shift_a, grad_scale_a, grad_gate_a, grad_shift_m, grad_scale_m, grad_gate_m]
    ).reshape(all_steps.shape[0], w_ada.shape[1])
    grad_modulation = lax.all_to_all(sum_ranks(grad_mod_part, ranks), "dp", 0, 0, tiled=True)
    grad_ada = jnp.einsum(
        "lc,lm->cm", cond_half.astype(jnp.float32), grad_modulation, precision=highest
    )
    grad_cond = lax.psum(
        jnp.einsum("lm,cm->lc", grad_modulation, w_ada.astype(jnp.float32), precision=highest),
        "dp",
    ) * silu_slope(cond)
    grad_table = jnp.einsum("ln,lc->nc", one_hot.astype(jnp.float32), grad_cond, precision=highest)
    return (
        block_out[None],
        grad_input[None],
        grad_table,
        grad_ada,
        jnp.stack([grad_attn_w[:, j * owned : (j + 1) * owned] for j in range(3)]),
        grad_attn_w[:, 3 * owned :].T,
        grad_mlp_w[:, : w_fc1.shape[1]],
        grad_mlp_w[:, w_fc1.shape[1] :].T,
    )


def solution(mesh):
    return jax.shard_map(
        functools.partial(shards, mesh.shape["tensor"]),
        mesh=mesh,
        in_specs=(
            P("dp", "tensor", None),
            P("dp"),
            P("dp"),
            P(None, "tensor"),
            P("tensor", "dp"),
            P(None, "dp", "tensor"),
            P("tensor", "dp"),
            P("dp", "tensor"),
            P("tensor", "dp"),
            P("dp", "tensor", None),
        ),
        out_specs=(
            P("dp", "tensor", None),
            P("dp", "tensor", None),
            P(None, "tensor"),
            P("tensor", "dp"),
            P(None, "dp", "tensor"),
            P("tensor", "dp"),
            P("dp", "tensor"),
            P("tensor", "dp"),
        ),
        check_vma=False,
    )
```

```python
import math

import jax
import jax.numpy as jnp
from jax import lax
from jax.sharding import PartitionSpec as P


D = 1152
H = 16


norm_epsilon = 1e-06
gelu_factor = 0.7978845608028654
gelu_cubic = 0.044715


def norm_rows(rows):
    average = jnp.mean(rows, axis=-1, keepdims=True)
    centred = rows - average
    variance = jnp.mean(centred * centred, axis=-1, keepdims=True)
    inv_std = lax.rsqrt(variance + norm_epsilon)
    return (centred * inv_std, inv_std)


def norm_back(grad_normed, normed, inv_std):
    first = jnp.mean(grad_normed, axis=-1, keepdims=True)
    second = jnp.mean(grad_normed * normed, axis=-1, keepdims=True)
    return inv_std * (grad_normed - first - normed * second)


def gelu_value(pre):
    inner = gelu_factor * (pre + gelu_cubic * pre * pre * pre)
    return 0.5 * pre * (1.0 + jnp.tanh(inner))


def gelu_slope(pre):
    tangent = jnp.tanh(gelu_factor * (pre + gelu_cubic * pre * pre * pre))
    return 0.5 * (1.0 + tangent) + 0.5 * pre * (1.0 - tangent * tangent) * gelu_factor * (
        1.0 + 3.0 * gelu_cubic * pre * pre
    )


def silu_value(value):
    return value * jax.nn.sigmoid(value)


def silu_slope(value):
    sigma = jax.nn.sigmoid(value)
    return sigma * (1.0 + value * (1.0 - sigma))


def time_columns(steps_float, columns, width):
    half = width // 2
    index = jnp.where(columns < half, columns, columns - half).astype(jnp.float32)
    freqs = jnp.exp(-math.log(10000.0) * index / half)
    angles = steps_float[:, None] * freqs[None, :]
    return jnp.where(columns[None, :] < half, jnp.cos(angles), jnp.sin(angles))


def attend(queries, keys, values, score_scale):
    scores = (
        jnp.einsum("qhd,khd->hqk", queries, keys, preferred_element_type=jnp.float32) * score_scale
    )
    largest = jnp.max(scores, axis=-1, keepdims=True)
    log_total = largest + jnp.log(jnp.sum(jnp.exp(scores - largest), axis=-1, keepdims=True))
    probs = jnp.exp(scores - log_total).astype(jnp.bfloat16)
    mixed = jnp.einsum("hqk,khd->qhd", probs, values, preferred_element_type=jnp.float32)
    return (mixed.astype(jnp.bfloat16), log_total[:, :, 0])


def attend_back(queries, keys, values, mixed, grad_mixed, log_totals, score_scale):
    scores = (
        jnp.einsum("qhd,khd->hqk", queries, keys, preferred_element_type=jnp.float32) * score_scale
    )
    probs = jnp.exp(scores - log_totals[:, :, None])
    grad_values = jnp.einsum(
        "hqk,qhd->khd", probs.astype(jnp.bfloat16), grad_mixed, preferred_element_type=jnp.float32
    )
    grad_probs = jnp.einsum("qhd,khd->hqk", grad_mixed, values, preferred_element_type=jnp.float32)
    delta = jnp.sum(grad_mixed.astype(jnp.float32) * mixed.astype(jnp.float32), axis=-1)
    grad_scores = (
        probs * (grad_probs - jnp.swapaxes(delta, 0, 1)[:, :, None]) * score_scale
    ).astype(jnp.bfloat16)
    grad_queries = jnp.einsum("hqk,khd->qhd", grad_scores, keys, preferred_element_type=jnp.float32)
    grad_keys = jnp.einsum("hqk,qhd->khd", grad_scores, queries, preferred_element_type=jnp.float32)
    return (grad_queries, grad_keys, grad_values)


def from_rank(value, ranks, step):
    return lax.ppermute(value, "tensor", [(i, (i - step) % ranks) for i in range(ranks)])


def fetch_rest(rows, ranks):
    got = [from_rank(rows, ranks, step) for step in range(1, ranks)]
    return got[0] if ranks == 2 else jnp.concatenate(got, axis=0)


def return_rest(partial, ranks):
    size = partial.shape[0] // (ranks - 1)
    total = None
    for step in range(1, ranks):
        part = partial[(step - 1) * size : step * size].astype(jnp.bfloat16)
        part = from_rank(part, ranks, ranks - step).astype(jnp.float32)
        total = part if total is None else total + part
    return total


def sum_ranks(value, ranks):
    total = value
    for step in range(1, ranks):
        total = total + from_rank(value, ranks, step)
    return total


def spread(value, groups):
    return lax.all_to_all(jnp.tile(value, (groups, 1)), "dp", 0, 0, tiled=True)


def sum_groups(value, groups):
    rows, width = value.shape
    cut = value.reshape(rows, groups, width // groups).swapaxes(0, 1)
    got = lax.all_to_all(cut, "dp", 0, 0, tiled=True)
    whole = spread(jnp.sum(got, axis=0), groups)
    return whole.reshape(groups, rows, width // groups).swapaxes(0, 1).reshape(rows, width)


def dot(spec, left, right):
    return jnp.einsum(spec, left, right, preferred_element_type=jnp.float32)


def join(own, rest):
    return jnp.concatenate([own, rest], axis=0)


def shards(
    ranks, groups, latents_in, steps, labels, class_table, w_ada, w_qkv, w_proj, w_fc1, w_fc2, cotangent
):
    half = jnp.bfloat16
    rank = lax.axis_index("tensor")
    width = latents_in.shape[2]
    mine = latents_in.shape[1]
    owned = class_table.shape[1]
    head_size = D // H
    heads_here = owned // head_size
    score_scale = head_size ** (-0.5)
    highest = lax.Precision.HIGHEST
    marks = spread(jnp.stack([steps, labels], axis=1), groups)
    all_steps, all_labels = marks[:, 0], marks[:, 1]
    attn_w = lax.all_gather(
        jnp.concatenate([w_qkv[0], w_qkv[1], w_qkv[2], w_proj.T], axis=1),
        "dp",
        axis=0,
        tiled=True,
    )
    mlp_w = lax.all_gather(jnp.concatenate([w_fc1, w_fc2.T], axis=1), "dp", axis=0, tiled=True)
    qkv_full, proj_t = attn_w[:, : 3 * owned], attn_w[:, 3 * owned :]
    fc1_full, fc2_t = mlp_w[:, : w_fc1.shape[1]], mlp_w[:, w_fc1.shape[1] :]
    columns = rank * owned + jnp.arange(owned, dtype=jnp.int32)
    classes = jnp.arange(class_table.shape[0], dtype=jnp.int32)
    one_hot = (all_labels[:, None] == classes[None, :]).astype(half)
    cond = time_columns(all_steps.astype(jnp.float32), columns, D) + jnp.dot(
        one_hot, class_table, preferred_element_type=jnp.float32
    )
    cond_half = silu_value(cond).astype(half)
    mod_part = jnp.dot(cond_half, w_ada, preferred_element_type=jnp.float32)
    modulation = lax.all_to_all(sum_ranks(mod_part, ranks), "dp", 0, 0, tiled=True)
    modulation = modulation.reshape(6, width)
    shift_a, scale_a, gate_a = (modulation[0], modulation[1], modulation[2])
    shift_m, scale_m, gate_m = (modulation[3], modulation[4], modulation[5])
    rows_in = latents_in[0].astype(jnp.float32)
    normed_a, inv_a = norm_rows(rows_in)
    mod_a = (normed_a * (1.0 + scale_a) + shift_a).astype(half)
    rest_a = fetch_rest(mod_a, ranks)
    grad_out = cotangent[0].astype(jnp.float32)
    grad_mlp = (grad_out * gate_m).astype(half)
    grad_mlp, rest_a = lax.optimization_barrier((grad_mlp, rest_a))
    rest_grad_m = fetch_rest(grad_mlp, ranks)
    qkv_own = dot("td,dc->tc", mod_a, qkv_full).astype(half)
    qkv_rest = dot("td,dc->tc", rest_a, qkv_full).astype(half)
    projected = join(qkv_own, qkv_rest)
    tokens = projected.shape[0]
    queries = projected[:, :owned].reshape(tokens, heads_here, head_size)
    keys = projected[:, owned : 2 * owned].reshape(tokens, heads_here, head_size)
    values = projected[:, 2 * owned :].reshape(tokens, heads_here, head_size)
    mixed_rest, log_rest = attend(queries[mine:], keys, values, score_scale)
    mixed_rest_flat = mixed_rest.reshape(tokens - mine, owned)
    attn_rest = dot("tc,dc->td", mixed_rest_flat, proj_t).astype(half)
    attn_rest, rest_grad_m = lax.optimization_barrier((attn_rest, rest_grad_m))
    attn_away = return_rest(attn_rest, ranks)
    mixed_own, log_own = attend(queries[:mine], keys, values, score_scale)
    mixed_own_flat = mixed_own.reshape(mine, owned)
    attn_out = dot("tc,dc->td", mixed_own_flat, proj_t) + attn_away
    hidden = rows_in + gate_a * attn_out
    normed_m, inv_m = norm_rows(hidden)
    mod_m = (normed_m * (1.0 + scale_m) + shift_m).astype(half)
    rest_m = fetch_rest(mod_m, ranks)
    pre_own = dot("td,df->tf", mod_m, fc1_full)
    acts_own = gelu_value(pre_own).astype(half)
    grad_pre_own = (dot("td,df->tf", grad_mlp, fc2_t) * gelu_slope(pre_own)).astype(half)
    acts_own, grad_pre_own, rest_m = lax.optimization_barrier((acts_own, grad_pre_own, rest_m))
    pre_rest = dot("td,df->tf", rest_m, fc1_full)
    acts_rest = gelu_value(pre_rest).astype(half)
    grad_pre_rest = (dot("td,df->tf", rest_grad_m, fc2_t) * gelu_slope(pre_rest)).astype(half)
    grad_mod_rest = dot("tf,df->td", grad_pre_rest, fc1_full).astype(half)
    grad_mod_rest, acts_rest = lax.optimization_barrier((grad_mod_rest, acts_rest))
    grad_mod_away = return_rest(grad_mod_rest, ranks)
    mlp_rest = dot("tf,df->td", acts_rest, fc2_t).astype(half)
    mlp_away = return_rest(mlp_rest, ranks)
    mlp_out = dot("tf,df->td", acts_own, fc2_t) + mlp_away
    grad_mod_m = dot("tf,df->td", grad_pre_own, fc1_full) + grad_mod_away
    grad_fc2_t = dot("td,tf->df", join(grad_mlp, rest_grad_m), join(acts_own, acts_rest))
    grad_fc1 = dot("td,tf->df", join(mod_m, rest_m), join(grad_pre_own, grad_pre_rest))
    mlp_w_part = jnp.concatenate([grad_fc1.astype(half), grad_fc2_t.astype(half)], axis=1)
    mlp_w_part, grad_mod_m = lax.optimization_barrier((mlp_w_part, grad_mod_m))
    grad_mlp_w = lax.psum_scatter(
        mlp_w_part,
        "dp",
        scatter_dimension=0,
        tiled=True,
    ).astype(jnp.float32)
    block_out = (hidden + gate_m * mlp_out).astype(half)
    grad_gate_m = jnp.sum(grad_out * mlp_out, axis=0)
    grad_shift_m = jnp.sum(grad_mod_m, axis=0)
    grad_scale_m = jnp.sum(grad_mod_m * normed_m, axis=0)
    grad_hidden = grad_out + norm_back(grad_mod_m * (1.0 + scale_m), normed_m, inv_m)
    grad_gate_a = jnp.sum(grad_hidden * attn_out, axis=0)
    grad_attn = (grad_hidden * gate_a).astype(half)
    rest_grad_a = fetch_rest(grad_attn, ranks)
    grad_mixed_own = dot("td,dc->tc", grad_attn, proj_t).astype(half)
    grad_mixed_rest = dot("td,dc->tc", rest_grad_a, proj_t).astype(half)
    mixed_flat = join(mixed_own_flat, mixed_rest_flat)
    grad_proj_t = dot("td,tc->dc", join(grad_attn, rest_grad_a), mixed_flat)
    grad_mixed = join(grad_mixed_own, grad_mixed_rest)
    grads = attend_back(
        queries,
        keys,
        values,
        mixed_flat.reshape(tokens, heads_here, head_size),
        grad_mixed.reshape(tokens, heads_here, head_size),
        jnp.concatenate([log_own, log_rest], axis=1),
        score_scale,
    )
    grad_qkv = jnp.concatenate([g.astype(half).reshape(tokens, owned) for g in grads], axis=1)
    grad_a_away = return_rest(dot("tc,dc->td", grad_qkv[mine:], qkv_full), ranks)
    grad_w_qkv = dot("td,tc->dc", join(mod_a, rest_a), grad_qkv)
    attn_w_part = jnp.concatenate([grad_w_qkv.astype(half), grad_proj_t.astype(half)], axis=1)
    attn_w_part, grad_mlp_w = lax.optimization_barrier((attn_w_part, grad_mlp_w))
    grad_attn_w = lax.psum_scatter(
        attn_w_part,
        "dp",
        scatter_dimension=0,
        tiled=True,
    ).astype(jnp.float32)
    grad_mod_a = dot("tc,dc->td", grad_qkv[:mine], qkv_full) + grad_a_away
    grad_shift_a = jnp.sum(grad_mod_a, axis=0)
    grad_scale_a = jnp.sum(grad_mod_a * normed_a, axis=0)
    grad_input = grad_hidden + norm_back(grad_mod_a * (1.0 + scale_a), normed_a, inv_a)
    grad_mod_part = jnp.stack(
        [grad_shift_a, grad_scale_a, grad_gate_a, grad_shift_m, grad_scale_m, grad_gate_m]
    ).reshape(all_steps.shape[0], w_ada.shape[1])
    grad_modulation = lax.all_to_all(sum_ranks(grad_mod_part, ranks), "dp", 0, 0, tiled=True)
    grad_ada = jnp.einsum(
        "lc,lm->cm", cond_half.astype(jnp.float32), grad_modulation, precision=highest
    )
    grad_cond = sum_groups(
        jnp.einsum("lm,cm->lc", grad_modulation, w_ada.astype(jnp.float32), precision=highest),
        groups,
    ) * silu_slope(cond)
    grad_table = jnp.einsum("ln,lc->nc", one_hot.astype(jnp.float32), grad_cond, precision=highest)
    return (
        block_out[None],
        grad_input[None],
        grad_table,
        grad_ada,
        jnp.stack([grad_attn_w[:, j * owned : (j + 1) * owned] for j in range(3)]),
        grad_attn_w[:, 3 * owned :].T,
        grad_mlp_w[:, : w_fc1.shape[1]],
        grad_mlp_w[:, w_fc1.shape[1] :].T,
    )


def solution(mesh):
    def body(*operands):
        return shards(mesh.shape["tensor"], mesh.shape["dp"], *operands)

    return jax.shard_map(
        body,
        mesh=mesh,
        in_specs=(
            P("dp", "tensor", None),
            P("dp"),
            P("dp"),
            P(None, "tensor"),
            P("tensor", "dp"),
            P(None, "dp", "tensor"),
            P("tensor", "dp"),
            P("dp", "tensor"),
            P("tensor", "dp"),
            P("dp", "tensor", None),
        ),
        out_specs=(
            P("dp", "tensor", None),
            P("dp", "tensor", None),
            P(None, "tensor"),
            P("tensor", "dp"),
            P(None, "dp", "tensor"),
            P("tensor", "dp"),
            P("dp", "tensor"),
            P("tensor", "dp"),
        ),
        check_vma=False,
    )
```
